768 devices in a mesh: energy: 32 (over y, x), atom: 24 (over z, core).
Axes of the slice: x: 4, y: 8, z: 12, core: 2. Of those that a mesh axis runs over, the one named last changes fastest.
Arguments:
- green_ret: bfloat16 [2, 12, 12, 1536, 768], P(None, None, None, ('energy', 'atom')), may hold values from -1.59375 to 1.59375
- broadening: bfloat16 [2, 2, 12, 12, 1536, 768], P(None, None, None, None, ('energy', 'atom')), may hold values from -6 to 6
- coupling: float32 [64], replicated, may hold values from 0.01 to 0.1
- occupation: float32 [64], replicated, may hold values from 0.05 to 3
- shifts: int32 [64], replicated, may hold values from 1 to 2, as said below
- neighbours: int32 [768, 34], P('atom'), may hold values from -24 to 791, as said below
- bond_count: int32 [768], P('atom'), may hold values from 17 to 34
- bond_weight: bfloat16 [768, 34], P('atom'), may hold values from -1 to 1
Outputs:
- self_energy: bfloat16 [2, 2, 12, 12, 1536, 768], P(None, None, None, None, ('energy', 'atom'))
- polarization: float32 [64, 768], P('energy', 'atom')
The draws below stay inside these ranges and needn't reach their ends.
Inputs may be any that keep to these rules, and one draw needn't show every extreme that they name: `shifts`: each mode's energy in energy steps. `neighbours`: the entries of row a are distinct and lie within 24 of a; entries outside 0 .. 767 name no atom. `bond_count`: the live slots of an atom are the leading ones of its row.
All inputs are finite; a program needn't handle non-finite values.
Results may differ from the reference program's by a relative error of at most 0.0076.
Values may be sent and summed in bfloat16 or wider, within the bound.
No kernel may reach another device: no remote copies, remote signals or barrier semaphores. Data moves between devices by JAX's collectives and lax.ppermute only.
A program may use at most 128 MiB of HBM per device.

```python
import math
import jax
import jax.numpy as jnp
from jax import lax

ORB = 12
NEIGH = 34
REACH = 24
MODES = 64
SHIFT = 2
NE = 1536
NA = 768


def draw_shifts(key, part):
    values = jax.random.randint(key, (MODES,), 1, SHIFT + 1)
    top_slot = jax.random.randint(jax.random.fold_in(key, 11), (), 0, MODES)
    values = values.at[top_slot].set(SHIFT)
    values = values.at[(top_slot + 1) % MODES].set(1)
    return values.astype(jnp.int32)


def draw_neighbours(key, part):
    width_all = 2 * REACH + 1
    scores = jax.random.randint(key, (NA, width_all), 0, 1 << 20) * width_all
    scores = scores + jnp.arange(width_all, dtype=jnp.int32)[None, :]
    scores = scores.at[0, 0].set(-1)
    scores = scores.at[NA - 1, width_all - 1].set(-1)
    middle = jax.random.randint(jax.random.fold_in(key, 7), (), 0, NA)
    scores = scores.at[middle, width_all - 1].set(-1)
    order = jnp.argsort(scores, axis=1, stable=True).astype(jnp.int32)
    offsets = order[:, :NEIGH] - REACH
    return (jnp.arange(NA, dtype=jnp.int32)[:, None] + offsets).astype(jnp.int32)


def touch_ends(drawn, own_key, low, high):
    spot = [jax.random.randint(jax.random.fold_in(own_key, axis), (), 0, length) for axis, length in enumerate(drawn.shape)]
    main_axis = drawn.shape.index(max(drawn.shape))
    neighbour = spot[:main_axis] + [(spot[main_axis] + 1) % drawn.shape[main_axis]] + spot[main_axis + 1:]
    return drawn.at[tuple(spot)].set(low).at[tuple(neighbour)].set(high)


def level_of(rng, dims, shards, smallest, largest):
    factor_of, own = 1.0, jax.random.fold_in(rng, 6)
    for position, blocks in shards:
        heights = jnp.exp(jax.random.uniform(jax.random.fold_in(own, position), (blocks,), jnp.float32, smallest / len(shards), largest / len(shards)))
        factor_of = factor_of * jnp.repeat(heights, dims[position] // blocks).reshape([-1 if axis == position else 1 for axis in range(len(dims))])
    return factor_of


def normal_values(stream_key, shape, width, limit, split=(), kind=jnp.bfloat16):
    drawn = width * jax.random.normal(stream_key, shape, jnp.float32)
    if split:
        drawn = drawn * level_of(stream_key, shape, split, -0.22, 0.18)
    return jnp.clip(drawn, -limit, limit).astype(kind)


def setup_inputs(seed: int = 0) -> dict:
    key_of = jax.random.split(jax.random.key(seed), 9)
    return {
        "green_ret": normal_values(key_of[0], (2, ORB, ORB, NE, NA), 0.2, 1.59375, ((3, 768),)),
        "broadening": normal_values(key_of[1], (2, 2, ORB, ORB, NE, NA), 1.0, 6.0, ((4, 768),)),
        "coupling": jnp.clip(jnp.exp(jax.random.uniform(key_of[2], (MODES,), jnp.float32, math.log(0.01), math.log(0.1))), 0.01, 0.1),
        "occupation": jnp.clip(jnp.exp(jax.random.uniform(key_of[3], (MODES,), jnp.float32, math.log(0.05), math.log(3.0))), 0.05, 3.0),
        "shifts": draw_shifts(jax.random.fold_in(key_of[8], 71), 0),
        "neighbours": draw_neighbours(jax.random.fold_in(key_of[8], 71), 0),
        "bond_count": touch_ends(jax.random.randint(key_of[6], (NA,), NEIGH // 2, NEIGH + 1), jax.random.fold_in(key_of[6], 1), NEIGH // 2, NEIGH).astype(jnp.int32),
        "bond_weight": normal_values(key_of[7], (NA, NEIGH), NEIGH ** -0.5, 1.0, ((0, 24),)),
    }


PRECISE = lax.Precision.HIGHEST

def complex_times(first, second):

    def product(one, two):
        return jnp.einsum('ikea,kjea->ijea', one, two, precision=PRECISE, preferred_element_type=jnp.float32)
    real_part = product(first[0], second[0]) - product(first[1], second[1])
    imag_part = product(first[0], second[1]) + product(first[1], second[0])
    return jnp.stack([real_part, imag_part])

def times_adjoint(first, second):

    def product(one, two):
        return jnp.einsum('ikea,jkea->ijea', one, two, precision=PRECISE, preferred_element_type=jnp.float32)
    real_part = product(first[0], second[0]) + product(first[1], second[1])
    imag_part = product(first[1], second[0]) - product(first[0], second[1])
    return jnp.stack([real_part, imag_part])

def reference(green_ret, broadening, coupling, occupation, shifts, neighbours, bond_count, bond_weight):
    retarded = green_ret.astype(jnp.float32)
    results = []
    for species in range(2):
        halfway = complex_times(retarded, broadening[species].astype(jnp.float32))
        results.append(times_adjoint(halfway, retarded))
    keldysh = jnp.stack(results).astype(jnp.bfloat16)
    levels = jnp.arange(1, SHIFT + 1, dtype=jnp.int32)
    onehot = (shifts[:, None] == levels[None, :]).astype(jnp.float32)
    emission16 = jnp.dot(coupling * (occupation + 1.0), onehot, precision=PRECISE).astype(jnp.bfloat16)
    absorption16 = jnp.dot(coupling * occupation, onehot, precision=PRECISE).astype(jnp.bfloat16)
    emission = lax.optimization_barrier(emission16).astype(jnp.float32)
    absorption = lax.optimization_barrier(absorption16).astype(jnp.float32)
    padded = jnp.pad(keldysh.astype(jnp.float32), [(0, 0)] * 4 + [(SHIFT, SHIFT), (0, 0)])
    lesser = jnp.zeros(keldysh.shape[1:], jnp.float32)
    greater = jnp.zeros(keldysh.shape[1:], jnp.float32)
    for offset in range(1, SHIFT + 1):
        higher = padded[:, :, :, :, SHIFT + offset:SHIFT + offset + NE]
        behind = padded[:, :, :, :, SHIFT - offset:SHIFT - offset + NE]
        lesser = lesser + emission[offset - 1] * higher[0] + absorption[offset - 1] * behind[0]
        greater = greater + absorption[offset - 1] * higher[1] + emission[offset - 1] * behind[1]
    shifted = jnp.stack([lesser, greater]).astype(jnp.bfloat16)
    atom_ids = jnp.arange(NA, dtype=jnp.int32)
    active = jnp.arange(NEIGH, dtype=jnp.int32)[None, :] < bond_count[:, None]
    weights = jnp.where(active, bond_weight.astype(jnp.float32), jnp.float32(0.0))
    matches = (neighbours[:, :, None] == atom_ids[None, None, :]).astype(jnp.float32)
    coupling_matrix = jnp.einsum('ak,akb->ab', weights, matches, precision=PRECISE)
    self_energy = jnp.einsum('kcijeb,ab->kcijea', shifted.astype(jnp.float32), coupling_matrix, precision=PRECISE).astype(jnp.bfloat16)
    lower = jnp.pad(keldysh[1].astype(jnp.float32), [(0, 0)] * 3 + [(SHIFT, 0), (0, 0)])
    parity = jnp.array([1.0, -1.0], jnp.float32).reshape(2, 1, 1, 1, 1)
    signed = keldysh[0].astype(jnp.float32) * parity
    totals = []
    for offset in range(1, SHIFT + 1):
        before = lower[:, :, :, SHIFT - offset:SHIFT - offset + NE]
        totals.append(jnp.einsum('cijea,cjiea->a', signed, before, precision=PRECISE))
    traces = jnp.stack(totals)
    polarization = coupling[:, None] * jnp.dot(onehot, traces, precision=PRECISE) / math.sqrt(NE)
    return (self_energy, polarization)
```

```python
import functools
import math

import jax
import jax.numpy as jnp
from jax import lax
from jax.experimental import pallas as pl
from jax.experimental.pallas import tpu as pltpu
from jax.sharding import PartitionSpec as P

REACH = 24
SHIFT = 2
ORB = 12
TILES = 6
ROWS = 12
BOTH = ("energy", "atom")
F32 = jnp.float32
BF16 = jnp.bfloat16
PRECISE = lax.Precision.HIGHEST


def natural(x):
    lead = x.shape[:-4]
    x = x.reshape(*lead, ORB, ORB, 2, TILES, 128)
    x = jnp.swapaxes(x, -3, -2)
    return x.reshape(*lead, ORB * ORB * ROWS, 128)


def from_natural(x):
    lead = x.shape[:-2]
    x = x.reshape(*lead, ORB, ORB, TILES, 2, 128)
    x = jnp.swapaxes(x, -3, -2)
    return x.reshape(*lead, ORB, ORB, 2, TILES * 128)


def low_half():
    return lax.broadcasted_iota(jnp.int32, (8, 128), 0) < 4


def turned(v):
    return pltpu.roll(v, 4, 0)


def doubled(v0, v1, v2, low):
    r0, r1, r2 = turned(v0), turned(v1), turned(v2)
    first = (v0, jnp.where(low, v1, r0), jnp.where(low, r0, r1))
    second = (jnp.where(low, r1, r2), jnp.where(low, r2, v1), v2)
    return first, second


def keldysh_kernel(first_row, rows, g_ref, b_ref, out_ref, gd, bn, hd, kn):
    low = low_half()

    def prepare(q, carry):
        start = pl.multiple_of(q * 48, 48)
        for c in range(2):
            x = g_ref[c, pl.ds(start, 48), :].astype(F32)
            y = b_ref[0, c, pl.ds(start, 48), :].astype(F32)
            for half in range(2):
                v = [x[24 * half + 8 * m : 24 * half + 8 * m + 8] for m in range(3)]
                for e, copy in enumerate(doubled(*v, low)):
                    for m in range(3):
                        gd[c, (q * 4 + half * 2 + e) * 3 + m] = copy[m]
            for m in range(6):
                bn[c, q * 6 + m] = y[8 * m : 8 * m + 8]
        return carry

    lax.fori_loop(0, 36, prepare, 0)

    def stage_one(step, carry):
        il = step // 3
        jb = step % 3
        re = [[[None] * 3 for _ in range(2)] for _ in range(2)]
        im = [[[None] * 3 for _ in range(2)] for _ in range(2)]
        for k in range(ORB):
            a = [
                [[gd[c, ((first_row + il * 2 + i) * ORB + k) * 3 + m] for m in range(3)] for i in range(2)]
                for c in range(2)
            ]
            b = [
                [[bn[c, (k * 6 + jb * 2 + p) * 3 + m] for m in range(3)] for p in range(2)]
                for c in range(2)
            ]
            for i in range(2):
                for p in range(2):
                    for m in range(3):
                        ar, ai = a[0][i][m], a[1][i][m]
                        br, bi = b[0][p][m], b[1][p][m]
                        if k == 0:
                            re[i][p][m] = ar * br - ai * bi
                            im[i][p][m] = ar * bi + ai * br
                        else:
                            re[i][p][m] = re[i][p][m] + ar * br - ai * bi
                            im[i][p][m] = im[i][p][m] + ar * bi + ai * br
        for i in range(2):
            for p in range(2):
                for c, value in ((0, re), (1, im)):
                    for e, copy in enumerate(doubled(*value[i][p], low)):
                        for m in range(3):
                            hd[c, ((il * 2 + i) * ORB + (jb * 2 + p) * 2 + e) * 3 + m] = copy[m]
        return carry

    lax.fori_loop(0, (rows // 2) * 3, stage_one, 0)

    def stage_two(step, carry):
        il = step // 3
        jb = step % 3
        re = [[[None] * 3 for _ in range(2)] for _ in range(2)]
        im = [[[None] * 3 for _ in range(2)] for _ in range(2)]
        for k in range(ORB):
            a = [
                [[hd[c, ((il * 2 + i) * ORB + k) * 3 + m] for m in range(3)] for i in range(2)]
                for c in range(2)
            ]
            b = []
            for c in range(2):
                pairs = []
                for p in range(2):
                    j0 = ((jb * 4 + p * 2) * ORB + k) * 3
                    j1 = j0 + ORB * 3
                    pairs.append(
                        (gd[c, j0], jnp.where(low, gd[c, j0 + 1], gd[c, j1 + 1]), gd[c, j1 + 2])
                    )
                b.append(pairs)
            for i in range(2):
                for p in range(2):
                    for m in range(3):
                        ar, ai = a[0][i][m], a[1][i][m]
                        br, bi = b[0][p][m], b[1][p][m]
                        if k == 0:
                            re[i][p][m] = ar * br + ai * bi
                            im[i][p][m] = ai * br - ar * bi
                        else:
                            re[i][p][m] = re[i][p][m] + ar * br + ai * bi
                            im[i][p][m] = im[i][p][m] + ai * br - ar * bi
        for i in range(2):
            for p in range(2):
                for c, value in ((0, re), (1, im)):
                    for m in range(3):
                        row = (c * rows * ORB * ROWS) + (
                            ((il * 2 + i) * 6 + jb * 2 + p) * 3 + m
                        ) * 8
                        kn[pl.ds(pl.multiple_of(row, 8), 8), :] = value[i][p][m]
        return carry

    lax.fori_loop(0, (rows // 2) * 3, stage_two, 0)

    count = 2 * rows * ORB
    for te in range(ROWS):
        out_ref[te] = kn[pl.ds(te, count, stride=ROWS), :].astype(BF16)


def keldysh(green, broad, species, first_row, rows):
    count = 2 * rows * ORB
    flops = 2 * 8 * rows * 144 * 1536
    return pl.pallas_call(
        functools.partial(keldysh_kernel, first_row, rows),
        grid=(1,),
        in_specs=[
            pl.BlockSpec((2, 1728, 128), lambda n: (0, 0, 0)),
            pl.BlockSpec((1, 2, 1728, 128), lambda n: (species, 0, 0, 0)),
        ],
        out_specs=pl.BlockSpec((ROWS, count, 128), lambda n: (0, 0, 0)),
        out_shape=jax.ShapeDtypeStruct((ROWS, count, 128), BF16),
        scratch_shapes=[
            pltpu.VMEM((2, 432, 8, 128), F32),
            pltpu.VMEM((2, 216, 8, 128), F32),
            pltpu.VMEM((2, rows * 36, 8, 128), F32),
            pltpu.VMEM((count * ROWS, 128), F32),
        ],
        cost_estimate=pl.CostEstimate(
            flops=flops, bytes_accessed=3 * 884736, transcendentals=0
        ),
        name="keldysh",
    )(green, broad)


def bonds_kernel(table_ref, out_ref, wide):
    lane = lax.broadcasted_iota(jnp.int32, (64, 128), 1)
    for t in range(TILES):
        x = table_ref[pl.ds(64 * t, 64), :].astype(F32)
        for odd in range(2):
            kept = jnp.where((lane >= 64) if odd else (lane < 64), x, 0.0)
            kept = jnp.concatenate([kept, jnp.zeros((64, 256), F32)], axis=1)
            start = 128 - REACH + (1 - 64 if odd else 0)
            kept = pltpu.roll(kept, 0, 1, stride=2, stride_axis=0)
            kept = pltpu.roll(kept, start, 1)
            for w in range(3):
                wide[w, pl.ds(odd, 64, stride=2), :] = kept[:, 128 * w : 128 * w + 128]
        for w in range(3):
            out_ref[t, :, 128 * w : 128 * w + 128] = wide[w].astype(BF16)


def bonds(table):
    return pl.pallas_call(
        bonds_kernel,
        out_shape=jax.ShapeDtypeStruct((TILES, 128, 384), BF16),
        in_specs=[pl.BlockSpec(memory_space=pltpu.VMEM)],
        out_specs=pl.BlockSpec(memory_space=pltpu.VMEM),
        scratch_shapes=[pltpu.VMEM((3, 128, 128), F32)],
        cost_estimate=pl.CostEstimate(flops=10**6, bytes_accessed=10**6, transcendentals=0),
        name="bonds",
    )(table)


def scatter_kernel(rows, *refs):
    c_ref, k_ref, a_ref, b_ref, w_ref = refs[:5]
    out_ref, mixed, back = refs[-3:]
    count = 2 * rows * ORB
    up1, dn1 = c_ref[0], c_ref[1]
    a00, a01, a10, a11 = c_ref[2], c_ref[3], c_ref[4], c_ref[5]
    b00, b01, b10, b11 = c_ref[6], c_ref[7], c_ref[8], c_ref[9]

    for t in range(TILES):
        k0 = k_ref[2 * t].astype(F32)
        k1 = k_ref[2 * t + 1].astype(F32)
        a0 = a_ref[2 * t].astype(F32)
        a1 = a_ref[2 * t + 1].astype(F32)
        b0 = b_ref[2 * t].astype(F32)
        b1 = b_ref[2 * t + 1].astype(F32)
        s0 = up1 * k1 + a00 * a0 + a01 * a1 + b00 * b0 + b01 * b1
        s1 = dn1 * k0 + a10 * a0 + a11 * a1 + b10 * b0 + b11 * b1
        mixed[0:count, 128 * t : 128 * t + 128] = s0.astype(BF16)
        mixed[count : 2 * count, 128 * t : 128 * t + 128] = s1.astype(BF16)
    for t in range(TILES):
        lo = max(0, t - 1)
        hi = min(TILES, t + 2)
        skip = lo - (t - 1)
        x = mixed[:, 128 * lo : 128 * hi]
        w = w_ref[t, :, 128 * skip : 128 * (skip + hi - lo)]
        y = lax.dot_general(x, w, (((1,), (1,)), ((), ())), preferred_element_type=F32)
        back[pl.ds(2 * t, count, stride=ROWS), :] = y[0:count]
        back[pl.ds(2 * t + 1, count, stride=ROWS), :] = y[count : 2 * count]
    half = rows * ORB * ROWS
    out_ref[0, 0] = back[0:half].astype(BF16)
    out_ref[0, 1] = back[half : 2 * half].astype(BF16)


def scattered(coefs, own, even, odd, weights, species, first_row, rows, target):
    count = 2 * rows * ORB
    vmem = pl.BlockSpec(memory_space=pltpu.VMEM)
    whole = pl.BlockSpec((ROWS, count, 128), lambda n: (0, 0, 0))
    operands = [coefs, own, even, odd, weights]
    in_specs = [
        pl.BlockSpec(memory_space=pltpu.SMEM),
        whole,
        whole,
        whole,
        pl.BlockSpec((TILES, 128, 384), lambda n: (0, 0, 0)),
    ]
    aliases = {}
    if target is not None:
        operands.append(target)
        in_specs.append(pl.BlockSpec(memory_space=pl.ANY))
        aliases = {5: 0}
    block = first_row // rows
    return pl.pallas_call(
        functools.partial(scatter_kernel, rows),
        grid=(1,),
        in_specs=in_specs,
        out_specs=pl.BlockSpec(
            (1, 2, rows * ORB * ROWS, 128), lambda n: (species, 0, block, 0)
        ),
        out_shape=jax.ShapeDtypeStruct((2, 2, 1728, 128), BF16),
        scratch_shapes=[
            pltpu.VMEM((2 * count, 768), BF16),
            pltpu.VMEM((count * ROWS, 128), F32),
        ],
        input_output_aliases=aliases,
        cost_estimate=pl.CostEstimate(
            flops=4 * count * 384 * 768, bytes_accessed=4 * count * ROWS * 256, transcendentals=0
        ),
        name="scattered",
    )(*operands)


def trace_kernel(pieces, c_ref, *refs):
    lesser = refs[: len(pieces)]
    greater = refs[len(pieces) : 2 * len(pieces)]
    even = refs[2 * len(pieces) : 3 * len(pieces)]
    odd = refs[3 * len(pieces) : 4 * len(pieces)]
    out_ref, ks, gs, ps = refs[-4:]
    from_even, from_odd = c_ref[10], c_ref[11]

    for t in range(TILES):
        for n, (first_row, rows) in enumerate(pieces):
            span = rows * ORB
            for e in range(2):
                k = lesser[n][2 * t + e].astype(F32)
                g = greater[n][2 * t + e].astype(F32)
                p = from_even * even[n][2 * t + e].astype(F32) + from_odd * odd[n][
                    2 * t + e
                ].astype(F32)
                for c in range(2):
                    at = c * 144 + first_row * ORB
                    ks[e, at : at + span] = k[c * span : c * span + span]
                    gs[e, at : at + span] = g[c * span : c * span + span]
                    ps[e, at : at + span] = p[c * span : c * span + span]
        one = jnp.zeros((ORB, 128), F32)
        two = jnp.zeros((ORB, 128), F32)
        for c in range(2):
            for i in range(ORB):
                at = c * 144 + ORB * i
                k0 = ks[0, pl.ds(at, ORB), :]
                k1 = ks[1, pl.ds(at, ORB), :]
                g0 = gs[0, pl.ds(c * 144 + i, ORB, stride=ORB), :]
                p0 = ps[0, pl.ds(c * 144 + i, ORB, stride=ORB), :]
                p1 = ps[1, pl.ds(c * 144 + i, ORB, stride=ORB), :]
                first = k0 * p1 + k1 * g0
                second = k0 * p0 + k1 * p1
                if c == 0:
                    one, two = one + first, two + second
                else:
                    one, two = one - first, two - second
        out_ref[0, t : t + 1] = jnp.sum(one, axis=0, keepdims=True)
        out_ref[1, t : t + 1] = jnp.sum(two, axis=0, keepdims=True)


def traced(coefs, pieces, lesser, greater, even, odd):
    vmem = pl.BlockSpec(memory_space=pltpu.VMEM)
    return pl.pallas_call(
        functools.partial(trace_kernel, pieces),
        out_shape=jax.ShapeDtypeStruct((2, TILES, 128), F32),
        in_specs=[pl.BlockSpec(memory_space=pltpu.SMEM)] + [vmem] * (4 * len(pieces)),
        out_specs=vmem,
        scratch_shapes=[pltpu.VMEM((2, 288, 128), F32)] * 3,
        cost_estimate=pl.CostEstimate(
            flops=8 * 288 * 1536, bytes_accessed=4 * 884736, transcendentals=0
        ),
        name="traced",
    )(coefs, *lesser, *greater, *even, *odd)


def everyone(x, axis):
    length = lax.axis_size(axis)
    return lax.all_to_all(jnp.broadcast_to(x[None], (length, *x.shape)), axis, 0, 0, tiled=True)


def local(pieces, green_ret, broadening, coupling, occupation, shifts, neighbours, bond_count, bond_weight):
    tile_width = neighbours.shape[0]
    tiles = lax.axis_size("atom")
    devices = tiles * lax.axis_size("energy")
    total_energies = 2 * devices
    green = natural(green_ret)
    broad = natural(broadening)

    active = jnp.arange(neighbours.shape[1], dtype=jnp.int32)[None, :] < bond_count[:, None]
    weights = jnp.where(active, bond_weight.astype(F32), 0.0)
    own_atoms = lax.axis_index("atom") * tile_width + jnp.arange(tile_width, dtype=jnp.int32)
    offset = neighbours - own_atoms[:, None] + REACH
    lanes = jnp.arange(64, dtype=jnp.int32)
    table = jnp.sum(
        jnp.where(offset[:, :, None] == lanes[None, None, :], weights[:, :, None], 0.0), axis=1
    ).astype(BF16)
    tables = everyone(table.reshape(tile_width // 2, 128), "atom")

    levels = jnp.arange(1, SHIFT + 1, dtype=jnp.int32)
    onehot = (shifts[:, None] == levels[None, :]).astype(F32)
    emission = jnp.dot(coupling * (occupation + 1.0), onehot, precision=PRECISE)
    absorption = jnp.dot(coupling * occupation, onehot, precision=PRECISE)
    emission = lax.reduce_precision(emission, 8, 7)
    absorption = lax.reduce_precision(absorption, 8, 7)
    parity = lax.axis_index("atom") % 2
    is_even = parity == 0

    def coefs_of(up, down):
        zero = jnp.zeros((), F32)
        nxt = jnp.stack([up[1], zero, up[0], up[1]])
        prv = jnp.stack([down[1], down[0], zero, down[1]])
        a = jnp.where(is_even, nxt, prv)
        b = jnp.where(is_even, prv, nxt)
        own = jnp.stack([up[0], down[0]])
        pick = jnp.where(is_even, jnp.array([0.0, 1.0], F32), jnp.array([1.0, 0.0], F32))
        return jnp.concatenate([own, a, b, pick, jnp.zeros((4,), F32)])

    coefs = (coefs_of(emission, absorption), coefs_of(absorption, emission))

    swap_even = [(i, i ^ 1) for i in range(devices)]
    swap_odd = [(i, i + 1) for i in range(1, devices - 1, 2)]
    swap_odd = swap_odd + [(target, source) for source, target in swap_odd]

    own = {}
    even = {}
    odd = {}
    for species in (1, 0):
        for piece in pieces:
            key = (species, piece)
            own[key] = keldysh(green, broad, species, *piece)
            odd[key] = lax.ppermute(own[key], BOTH, swap_odd)
            even[key] = lax.ppermute(own[key], BOTH, swap_even)
    weights_band = bonds(tables.reshape(tiles * tile_width // 2, 128))

    traces = traced(
        coefs[1],
        pieces,
        [own[0, piece] for piece in pieces],
        [own[1, piece] for piece in pieces],
        [even[1, piece] for piece in pieces],
        [odd[1, piece] for piece in pieces],
    )
    shares = traces.reshape(2, tiles, tile_width)
    shares = jnp.swapaxes(shares, 0, 1).reshape(tiles, 1, 2 * tile_width)
    shares = lax.all_to_all(shares, "atom", 0, 0, tiled=True).sum(axis=0)
    total = everyone(shares, "energy").sum(axis=0).reshape(2, tile_width)
    share_rows = shifts.shape[0] // lax.axis_size("energy")
    first = lax.axis_index("energy") * share_rows
    own_onehot = lax.dynamic_slice_in_dim(onehot, first, share_rows, 0)
    own_coupling = lax.dynamic_slice_in_dim(coupling, first, share_rows, 0)
    picked = own_onehot[:, 0:1] * total[0:1] + own_onehot[:, 1:2] * total[1:2]
    polarization = own_coupling[:, None] * picked / math.sqrt(total_energies)

    result = None
    for species in (1, 0):
        for piece in pieces:
            key = (species, piece)
            result = scattered(
                coefs[species], own[key], even[key], odd[key], weights_band, species, *piece, result
            )
    return (from_natural(result), polarization)


def solution(mesh):
    in_specs = (
        P(None, None, None, ("energy", "atom"), None),
        P(None, None, None, None, ("energy", "atom"), None),
        P(),
        P(),
        P(),
        P("atom", None),
        P("atom"),
        P("atom", None),
    )
    out_specs = (P(None, None, None, None, ("energy", "atom"), None), P("energy", "atom"))
    pieces = ((0, 12),)
    return jax.shard_map(
        functools.partial(local, pieces), mesh=mesh, in_specs=in_specs, out_specs=out_specs, check_vma=False
    )
```

```python
import functools
import math

import jax
import jax.numpy as jnp
from jax import lax
from jax.experimental import pallas as pl
from jax.experimental.layout import Layout, with_layout_constraint
from jax.experimental.pallas import tpu as pltpu
from jax.sharding import PartitionSpec as P

REACH = 24
SHIFT = 2
ORB = 12
TILES = 6
ROWS = 12
BOTH = ("energy", "atom")
F32 = jnp.float32
BF16 = jnp.bfloat16
PRECISE = lax.Precision.HIGHEST


def natural(x):
    lead = x.shape[:-4]
    x = x.reshape(*lead, ORB, ORB, 2, TILES, 128)
    n = x.ndim
    order = tuple(range(n - 3)) + (n - 2, n - 3, n - 1)
    x = with_layout_constraint(x, Layout(major_to_minor=order))
    x = jnp.swapaxes(x, -3, -2)
    x = with_layout_constraint(x, Layout(major_to_minor=tuple(range(n))))
    return x.reshape(*lead, ORB * ORB * ROWS, 128)


def from_natural(x):
    lead = x.shape[:-2]
    x = x.reshape(*lead, ORB, ORB, TILES, 2, 128)
    n = x.ndim
    x = with_layout_constraint(x, Layout(major_to_minor=tuple(range(n))))
    x = jnp.swapaxes(x, -3, -2)
    order = tuple(range(n - 3)) + (n - 2, n - 3, n - 1)
    x = with_layout_constraint(x, Layout(major_to_minor=order))
    return x.reshape(*lead, ORB, ORB, 2, TILES * 128)


def low_half():
    return lax.broadcasted_iota(jnp.int32, (8, 128), 0) < 4


def turned(v):
    return pltpu.roll(v, 4, 0)


def doubled(v0, v1, v2, low):
    r0, r1, r2 = turned(v0), turned(v1), turned(v2)
    first = (v0, jnp.where(low, v1, r0), jnp.where(low, r0, r1))
    second = (jnp.where(low, r1, r2), jnp.where(low, r2, v1), v2)
    return first, second


def keldysh_kernel(first_row, rows, g_ref, b_ref, out_ref, gd, bn, hd, kn):
    low = low_half()

    def prepare(q, carry):
        start = pl.multiple_of(q * 48, 48)
        for c in range(2):
            x = g_ref[c, pl.ds(start, 48), :].astype(F32)
            y = b_ref[0, c, pl.ds(start, 48), :].astype(F32)
            for half in range(2):
                v = [x[24 * half + 8 * m : 24 * half + 8 * m + 8] for m in range(3)]
                for e, copy in enumerate(doubled(*v, low)):
                    for m in range(3):
                        gd[c, (q * 4 + half * 2 + e) * 3 + m] = copy[m]
            for m in range(6):
                bn[c, q * 6 + m] = y[8 * m : 8 * m + 8]
        return carry

    lax.fori_loop(0, 36, prepare, 0)

    def stage_one(step, carry):
        il = step // 3
        jb = step % 3
        re = [[[None] * 3 for _ in range(2)] for _ in range(2)]
        im = [[[None] * 3 for _ in range(2)] for _ in range(2)]
        for k in range(ORB):
            a = [
                [[gd[c, ((first_row + il * 2 + i) * ORB + k) * 3 + m] for m in range(3)] for i in range(2)]
                for c in range(2)
            ]
            b = [
                [[bn[c, (k * 6 + jb * 2 + p) * 3 + m] for m in range(3)] for p in range(2)]
                for c in range(2)
            ]
            for i in range(2):
                for p in range(2):
                    for m in range(3):
                        ar, ai = a[0][i][m], a[1][i][m]
                        br, bi = b[0][p][m], b[1][p][m]
                        if k == 0:
                            re[i][p][m] = ar * br - ai * bi
                            im[i][p][m] = ar * bi + ai * br
                        else:
                            re[i][p][m] = re[i][p][m] + ar * br - ai * bi
                            im[i][p][m] = im[i][p][m] + ar * bi + ai * br
        for i in range(2):
            for p in range(2):
                for c, value in ((0, re), (1, im)):
                    for e, copy in enumerate(doubled(*value[i][p], low)):
                        for m in range(3):
                            hd[c, ((il * 2 + i) * ORB + (jb * 2 + p) * 2 + e) * 3 + m] = copy[m]
        return carry

    lax.fori_loop(0, (rows // 2) * 3, stage_one, 0)

    def stage_two(step, carry):
        il = step // 3
        jb = step % 3
        re = [[[None] * 3 for _ in range(2)] for _ in range(2)]
        im = [[[None] * 3 for _ in range(2)] for _ in range(2)]
        for k in range(ORB):
            a = [
                [[hd[c, ((il * 2 + i) * ORB + k) * 3 + m] for m in range(3)] for i in range(2)]
                for c in range(2)
            ]
            b = []
            for c in range(2):
                pairs = []
                for p in range(2):
                    j0 = ((jb * 4 + p * 2) * ORB + k) * 3
                    j1 = j0 + ORB * 3
                    pairs.append(
                        (gd[c, j0], jnp.where(low, gd[c, j0 + 1], gd[c, j1 + 1]), gd[c, j1 + 2])
                    )
                b.append(pairs)
            for i in range(2):
                for p in range(2):
                    for m in range(3):
                        ar, ai = a[0][i][m], a[1][i][m]
                        br, bi = b[0][p][m], b[1][p][m]
                        if k == 0:
                            re[i][p][m] = ar * br + ai * bi
                            im[i][p][m] = ai * br - ar * bi
                        else:
                            re[i][p][m] = re[i][p][m] + ar * br + ai * bi
                            im[i][p][m] = im[i][p][m] + ai * br - ar * bi
        for i in range(2):
            for p in range(2):
                for c, value in ((0, re), (1, im)):
                    for m in range(3):
                        row = (c * rows * ORB * ROWS) + (
                            ((il * 2 + i) * 6 + jb * 2 + p) * 3 + m
                        ) * 8
                        kn[pl.ds(pl.multiple_of(row, 8), 8), :] = value[i][p][m]
        return carry

    lax.fori_loop(0, (rows // 2) * 3, stage_two, 0)

    count = 2 * rows * ORB
    for te in range(ROWS):
        out_ref[te] = kn[pl.ds(te, count, stride=ROWS), :].astype(BF16)


def keldysh(green, broad, species, first_row, rows):
    count = 2 * rows * ORB
    flops = 2 * 8 * rows * 144 * 1536
    return pl.pallas_call(
        functools.partial(keldysh_kernel, first_row, rows),
        grid=(1,),
        in_specs=[
            pl.BlockSpec((2, 1728, 128), lambda n: (0, 0, 0)),
            pl.BlockSpec((1, 2, 1728, 128), lambda n: (species, 0, 0, 0)),
        ],
        out_specs=pl.BlockSpec((ROWS, count, 128), lambda n: (0, 0, 0)),
        out_shape=jax.ShapeDtypeStruct((ROWS, count, 128), BF16),
        scratch_shapes=[
            pltpu.VMEM((2, 432, 8, 128), F32),
            pltpu.VMEM((2, 216, 8, 128), F32),
            pltpu.VMEM((2, rows * 36, 8, 128), F32),
            pltpu.VMEM((count * ROWS, 128), F32),
        ],
        cost_estimate=pl.CostEstimate(
            flops=flops, bytes_accessed=3 * 884736, transcendentals=0
        ),
        name="keldysh",
    )(green, broad)


def bonds_kernel(table_ref, out_ref, wide):
    lane = lax.broadcasted_iota(jnp.int32, (64, 128), 1)
    for t in range(TILES):
        x = table_ref[pl.ds(64 * t, 64), :].astype(F32)
        for odd in range(2):
            kept = jnp.where((lane >= 64) if odd else (lane < 64), x, 0.0)
            kept = jnp.concatenate([kept, jnp.zeros((64, 256), F32)], axis=1)
            start = 128 - REACH + (1 - 64 if odd else 0)
            kept = pltpu.roll(kept, 0, 1, stride=2, stride_axis=0)
            kept = pltpu.roll(kept, start, 1)
            for w in range(3):
                wide[w, pl.ds(odd, 64, stride=2), :] = kept[:, 128 * w : 128 * w + 128]
        for w in range(3):
            out_ref[t, :, 128 * w : 128 * w + 128] = wide[w].astype(BF16)


def bonds(table):
    return pl.pallas_call(
        bonds_kernel,
        out_shape=jax.ShapeDtypeStruct((TILES, 128, 384), BF16),
        in_specs=[pl.BlockSpec(memory_space=pltpu.VMEM)],
        out_specs=pl.BlockSpec(memory_space=pltpu.VMEM),
        scratch_shapes=[pltpu.VMEM((3, 128, 128), F32)],
        cost_estimate=pl.CostEstimate(flops=10**6, bytes_accessed=10**6, transcendentals=0),
        name="bonds",
    )(table)


def scatter_kernel(rows, *refs):
    c_ref, k_ref, a_ref, b_ref, w_ref = refs[:5]
    out_ref, mixed, back = refs[-3:]
    count = 2 * rows * ORB
    up1, dn1 = c_ref[0], c_ref[1]
    a00, a01, a10, a11 = c_ref[2], c_ref[3], c_ref[4], c_ref[5]
    b00, b01, b10, b11 = c_ref[6], c_ref[7], c_ref[8], c_ref[9]

    for t in range(TILES):
        k0 = k_ref[2 * t].astype(F32)
        k1 = k_ref[2 * t + 1].astype(F32)
        a0 = a_ref[2 * t].astype(F32)
        a1 = a_ref[2 * t + 1].astype(F32)
        b0 = b_ref[2 * t].astype(F32)
        b1 = b_ref[2 * t + 1].astype(F32)
        s0 = up1 * k1 + a00 * a0 + a01 * a1 + b00 * b0 + b01 * b1
        s1 = dn1 * k0 + a10 * a0 + a11 * a1 + b10 * b0 + b11 * b1
        mixed[0:count, 128 * t : 128 * t + 128] = s0.astype(BF16)
        mixed[count : 2 * count, 128 * t : 128 * t + 128] = s1.astype(BF16)
    for t in range(TILES):
        lo = max(0, t - 1)
        hi = min(TILES, t + 2)
        skip = lo - (t - 1)
        x = mixed[:, 128 * lo : 128 * hi]
        w = w_ref[t, :, 128 * skip : 128 * (skip + hi - lo)]
        y = lax.dot_general(x, w, (((1,), (1,)), ((), ())), preferred_element_type=F32)
        back[pl.ds(2 * t, count, stride=ROWS), :] = y[0:count]
        back[pl.ds(2 * t + 1, count, stride=ROWS), :] = y[count : 2 * count]
    half = rows * ORB * ROWS
    out_ref[0, 0] = back[0:half].astype(BF16)
    out_ref[0, 1] = back[half : 2 * half].astype(BF16)


def scattered(coefs, own, even, odd, weights, species, first_row, rows, target):
    count = 2 * rows * ORB
    vmem = pl.BlockSpec(memory_space=pltpu.VMEM)
    whole = pl.BlockSpec((ROWS, count, 128), lambda n: (0, 0, 0))
    operands = [coefs, own, even, odd, weights]
    in_specs = [
        pl.BlockSpec(memory_space=pltpu.SMEM),
        whole,
        whole,
        whole,
        pl.BlockSpec((TILES, 128, 384), lambda n: (0, 0, 0)),
    ]
    aliases = {}
    if target is not None:
        operands.append(target)
        in_specs.append(pl.BlockSpec(memory_space=pl.ANY))
        aliases = {5: 0}
    block = first_row // rows
    return pl.pallas_call(
        functools.partial(scatter_kernel, rows),
        grid=(1,),
        in_specs=in_specs,
        out_specs=pl.BlockSpec(
            (1, 2, rows * ORB * ROWS, 128), lambda n: (species, 0, block, 0)
        ),
        out_shape=jax.ShapeDtypeStruct((2, 2, 1728, 128), BF16),
        scratch_shapes=[
            pltpu.VMEM((2 * count, 768), BF16),
            pltpu.VMEM((count * ROWS, 128), F32),
        ],
        input_output_aliases=aliases,
        cost_estimate=pl.CostEstimate(
            flops=4 * count * 384 * 768, bytes_accessed=4 * count * ROWS * 256, transcendentals=0
        ),
        name="scattered",
    )(*operands)


def trace_kernel(pieces, c_ref, *refs):
    lesser = refs[: len(pieces)]
    greater = refs[len(pieces) : 2 * len(pieces)]
    even = refs[2 * len(pieces) : 3 * len(pieces)]
    odd = refs[3 * len(pieces) : 4 * len(pieces)]
    out_ref, ks, gs, ps = refs[-4:]
    from_even, from_odd = c_ref[10], c_ref[11]

    for t in range(TILES):
        for n, (first_row, rows) in enumerate(pieces):
            span = rows * ORB
            for e in range(2):
                k = lesser[n][2 * t + e].astype(F32)
                g = greater[n][2 * t + e].astype(F32)
                p = from_even * even[n][2 * t + e].astype(F32) + from_odd * odd[n][
                    2 * t + e
                ].astype(F32)
                for c in range(2):
                    at = c * 144 + first_row * ORB
                    ks[e, at : at + span] = k[c * span : c * span + span]
                    gs[e, at : at + span] = g[c * span : c * span + span]
                    ps[e, at : at + span] = p[c * span : c * span + span]
        one = jnp.zeros((ORB, 128), F32)
        two = jnp.zeros((ORB, 128), F32)
        for c in range(2):
            for i in range(ORB):
                at = c * 144 + ORB * i
                k0 = ks[0, pl.ds(at, ORB), :]
                k1 = ks[1, pl.ds(at, ORB), :]
                g0 = gs[0, pl.ds(c * 144 + i, ORB, stride=ORB), :]
                p0 = ps[0, pl.ds(c * 144 + i, ORB, stride=ORB), :]
                p1 = ps[1, pl.ds(c * 144 + i, ORB, stride=ORB), :]
                first = k0 * p1 + k1 * g0
                second = k0 * p0 + k1 * p1
                if c == 0:
                    one, two = one + first, two + second
                else:
                    one, two = one - first, two - second
        out_ref[0, t : t + 1] = jnp.sum(one, axis=0, keepdims=True)
        out_ref[1, t : t + 1] = jnp.sum(two, axis=0, keepdims=True)


def traced(coefs, pieces, lesser, greater, even, odd):
    vmem = pl.BlockSpec(memory_space=pltpu.VMEM)
    return pl.pallas_call(
        functools.partial(trace_kernel, pieces),
        out_shape=jax.ShapeDtypeStruct((2, TILES, 128), F32),
        in_specs=[pl.BlockSpec(memory_space=pltpu.SMEM)] + [vmem] * (4 * len(pieces)),
        out_specs=vmem,
        scratch_shapes=[pltpu.VMEM((2, 288, 128), F32)] * 3,
        cost_estimate=pl.CostEstimate(
            flops=8 * 288 * 1536, bytes_accessed=4 * 884736, transcendentals=0
        ),
        name="traced",
    )(coefs, *lesser, *greater, *even, *odd)


def everyone(x, axis):
    length = lax.axis_size(axis)
    return lax.all_to_all(jnp.broadcast_to(x[None], (length, *x.shape)), axis, 0, 0, tiled=True)


def local(pieces, green_ret, broadening, coupling, occupation, shifts, neighbours, bond_count, bond_weight):
    tile_width = neighbours.shape[0]
    tiles = lax.axis_size("atom")
    devices = tiles * lax.axis_size("energy")
    total_energies = 2 * devices
    green = natural(green_ret)
    broad = natural(broadening)

    active = jnp.arange(neighbours.shape[1], dtype=jnp.int32)[None, :] < bond_count[:, None]
    weights = jnp.where(active, bond_weight.astype(F32), 0.0)
    own_atoms = lax.axis_index("atom") * tile_width + jnp.arange(tile_width, dtype=jnp.int32)
    offset = neighbours - own_atoms[:, None] + REACH
    lanes = jnp.arange(64, dtype=jnp.int32)
    table = jnp.sum(
        jnp.where(offset[:, :, None] == lanes[None, None, :], weights[:, :, None], 0.0), axis=1
    ).astype(BF16)
    tables = everyone(table.reshape(tile_width // 2, 128), "atom")

    levels = jnp.arange(1, SHIFT + 1, dtype=jnp.int32)
    onehot = (shifts[:, None] == levels[None, :]).astype(F32)
    emit = coupling * (occupation + 1.0)
    absorb = coupling * occupation
    emission = lax.reduce_precision(jnp.sum(emit[:, None] * onehot, axis=0), 8, 7)
    absorption = lax.reduce_precision(jnp.sum(absorb[:, None] * onehot, axis=0), 8, 7)
    is_even = lax.axis_index("atom") % 2 == 0
    slot = jnp.arange(16, dtype=jnp.int32)

    def coefs_of(up, down):
        def at(*places):
            found = slot == places[0]
            for place in places[1:]:
                found = found | (slot == place)
            return found

        def either(even_places, odd_places):
            return jnp.where(is_even, at(*even_places), at(*odd_places))

        value = jnp.zeros((16,), F32)
        value = jnp.where(either((0, 4), (0, 8)), up[0], value)
        value = jnp.where(either((2, 5), (6, 9)), up[1], value)
        value = jnp.where(either((1, 7), (1, 3)), down[0], value)
        value = jnp.where(either((6, 9), (2, 5)), down[1], value)
        return jnp.where(either((11,), (10,)), 1.0, value)

    coefs = (coefs_of(emission, absorption), coefs_of(absorption, emission))

    swap_even = [(i, i ^ 1) for i in range(devices)]
    swap_odd = [(i, i + 1) for i in range(1, devices - 1, 2)]
    swap_odd = swap_odd + [(target, source) for source, target in swap_odd]

    own = {}
    even = {}
    odd = {}
    for species in (1, 0):
        for piece in pieces:
            key = (species, piece)
            own[key] = keldysh(green, broad, species, *piece)
            odd[key] = lax.ppermute(own[key], BOTH, swap_odd)
            even[key] = lax.ppermute(own[key], BOTH, swap_even)
    weights_band = bonds(tables.reshape(tiles * tile_width // 2, 128))

    traces = traced(
        coefs[1],
        pieces,
        [own[0, piece] for piece in pieces],
        [own[1, piece] for piece in pieces],
        [even[1, piece] for piece in pieces],
        [odd[1, piece] for piece in pieces],
    )
    shares = traces.reshape(2, tiles, tile_width)
    shares = jnp.swapaxes(shares, 0, 1).reshape(tiles, 1, 2 * tile_width)
    shares = lax.all_to_all(shares, "atom", 0, 0, tiled=True).sum(axis=0)
    total = everyone(shares, "energy").sum(axis=0).reshape(2, tile_width)
    share_rows = shifts.shape[0] // lax.axis_size("energy")
    first = lax.axis_index("energy") * share_rows
    own_onehot = lax.dynamic_slice_in_dim(onehot, first, share_rows, 0)
    own_coupling = lax.dynamic_slice_in_dim(coupling, first, share_rows, 0)
    picked = own_onehot[:, 0:1] * total[0:1] + own_onehot[:, 1:2] * total[1:2]
    polarization = own_coupling[:, None] * picked / math.sqrt(total_energies)

    result = None
    for species in (1, 0):
        for piece in pieces:
            key = (species, piece)
            result = scattered(
                coefs[species], own[key], even[key], odd[key], weights_band, species, *piece, result
            )
    return (from_natural(result), polarization)


def solution(mesh):
    in_specs = (
        P(None, None, None, ("energy", "atom"), None),
        P(None, None, None, None, ("energy", "atom"), None),
        P(),
        P(),
        P(),
        P("atom", None),
        P("atom"),
        P("atom", None),
    )
    out_specs = (P(None, None, None, None, ("energy", "atom"), None), P("energy", "atom"))
    pieces = ((0, 12),)
    return jax.shard_map(
        functools.partial(local, pieces), mesh=mesh, in_specs=in_specs, out_specs=out_specs, check_vma=False
    )
```
